32 devices in a mesh: grp: 2 (over y), chan: 4 (over z), sub: 4 (over x, core).
Axes of the slice: x: 2, y: 2, z: 4, core: 2. Of those that a mesh axis runs over, the one named last changes fastest.
Arguments:
- voltages: bfloat16 [2048, 2, 5504], P(('grp', 'chan', 'sub')), parts along dimension 0, may hold values from -6 to 6
- taps: float32 [1536], replicated, may hold values from -0.15625 to 0.15625
- input_id: int32 [1024], replicated, may hold values from 0 to 1023, each once
- counts: int32 [8], P('grp'), parts along dimension 0, may hold values from 2 to 8, as said below
- delays: int32 [512, 1024], P(('grp', 'sub')), parts along dimension 0, may hold values from 0 to 127
- beam_owner: int32 [512, 1], P('grp'), parts along dimension 0, may hold values from 0 to 3; in each aligned block of 64 rows (0 to 63, 64 to 127, ...) at most 32 rows name the same one
Outputs:
- visibility: bfloat16 [256, 2, 1024, 1024], P(('grp', 'chan'), None, 'sub'), parts along dimension 0
- resynth: float32 [1024, 2, 5504], P(('grp', 'chan', 'sub')), parts along dimension 0
The draws below stay inside these ranges and needn't reach their ends.
There are 2 independent parts, one for each index of `grp`. The reference program is written for one: setup_inputs(seed, part) draws one part's arguments, and reference() takes and returns one part's arrays. A program takes and returns all parts, laid end to end along the dimension named above; an argument that names none is the same for every part. Nothing has to cross between parts.
Inputs may be any that keep to these rules, and one draw needn't show every extreme that they name: `input_id`: each input id appears once. `counts`: every draw has a block with all 8 spectra valid. `beam_owner`: within each section of 64 consecutive beams no owner is named more than 32 times; some owner is named exactly 32 times in some section.
All inputs are finite; a program needn't handle non-finite values.
Results may differ from the reference program's by a relative error of at most 0.007.
Values may be sent and summed in bfloat16 or wider, within the bound.
A program may use at most 192 MiB of HBM per device.

```python
import math
import jax
import jax.numpy as jnp
import numpy as np
from jax import lax

INPUTS = 1024
NCH = 128
TAPS = 12
SPEC = 8
BLOCKS = 4
BEAMS = 256
NSPEC = 32
SAMPLES = 5504
BEAMS_SEC = 64
MOST = 32
SLOTS = 512
N_CHAN = 4
N_SUB = 4


def draw_counts(key, part):
    lowest = max(1, SPEC // 4)
    drawn = jax.random.randint(key, (BLOCKS,), lowest, SPEC + 1)
    chosen = jax.random.randint(jax.random.fold_in(key, 7), (), 0, BLOCKS)
    return jnp.where(jnp.arange(BLOCKS) == chosen, SPEC, drawn).astype(jnp.int32)


def plant(values, key, smallest, high):
    dims = values.shape
    place = [jax.random.randint(jax.random.fold_in(key, axis), (), 0, dims[axis]) for axis in range(len(dims))]
    values = values.at[tuple(place)].set(smallest)
    longest = dims.index(max(dims))
    place[longest] = (place[longest] + 1) % dims[longest]
    return values.at[tuple(place)].set(high)


def level_of(own_key, extent, cuts, low, high):
    def one(axis_at, blocks):
        heights = jax.random.uniform(jax.random.fold_in(jax.random.fold_in(own_key, 6), axis_at), (blocks,), jnp.float32, low / len(cuts), high / len(cuts))
        return jnp.repeat(jnp.exp(heights), extent[axis_at] // blocks).reshape((-1,) + (1,) * (len(extent) - axis_at - 1))

    factor_of = one(*cuts[0])
    for cut in cuts[1:]:
        factor_of = factor_of * one(*cut)
    return factor_of


def shared_out(rng, own, number, rows, count, top, bound, skew):
    order = jax.random.permutation(rng, count)
    crowded, usual = load_shares(count, rows * top, bound, skew, True), load_shares(count, rows * top, bound, skew, False)
    places = jnp.arange(count)

    def named(tallies, rotation):
        used = int((tallies > 0).sum())
        fixed = max(1, used // 4)
        shifted = fixed + (places - fixed + rotation * (used - fixed)) % max(1, count - fixed)
        return jnp.zeros((count,), jnp.int32).at[order[jnp.where(places < fixed, places, shifted)]].set(jnp.asarray(tallies, jnp.int32))

    tallies = jnp.where(number % 4 == 0, named(crowded, number // 4), named(usual, number - number // 4 - 1))
    mixed = jax.random.permutation(jax.random.fold_in(own, 3), count)
    donor, sink = mixed[0:count // 2 * 2:2], mixed[1:count // 2 * 2:2]
    slack = jnp.minimum(tallies[donor] - 1, bound - tallies[sink]) // 2
    slack = jnp.where((donor == order[0]) | (sink == order[0]) | (tallies[sink] == 0), 0, jnp.maximum(slack, 0))
    shifted = jax.random.randint(jax.random.fold_in(own, 4), (count // 2,), 0, 1 << 20) % (slack + 1)
    tallies = tallies.at[donor].add(-shifted).at[sink].add(shifted)
    members = jnp.searchsorted(jnp.cumsum(tallies), jnp.arange(rows * top), side="right").astype(jnp.int32)
    table = members.reshape(top, rows).T
    table = table[jax.random.permutation(jax.random.fold_in(own, 1), rows)]
    rotation = jax.random.randint(jax.random.fold_in(own, 2), (rows, 1), 0, top)
    return jnp.take_along_axis(table, (jnp.arange(top)[None, :] + rotation) % top, axis=1)


def load_shares(number_of, total, bound, skew, full):
    loads = [(1 << 20) // math.isqrt(standing ** skew) + 1 for standing in range(1, number_of + 1)]
    largest = bound if full else min(bound, max(-(-total // number_of), total * loads[0] // sum(loads)))
    least = 1 if total - largest >= number_of - 1 else 0
    holding, spare = [largest] + [least] * (number_of - 1), total - largest - least * (number_of - 1)
    while spare > 0:
        candidates = [i for i in range(1, number_of) if holding[i] < largest] or [i for i in range(1, number_of) if holding[i] < bound]
        whole, left = sum([loads[i] for i in candidates]), spare
        for i in candidates:
            more = min(bound - holding[i], max(1, left * loads[i] // whole), spare)
            holding[i] = holding[i] + more
            spare = spare - more
    return np.array(holding)


def centred(stream_key, dims, deviation, most, pieces=(), held_as=jnp.bfloat16):
    loudness = level_of(stream_key, dims, pieces, -0.22, 0.18) if pieces else 1.0
    array = jax.random.normal(stream_key, dims, jnp.float32) * deviation * loudness
    return jnp.minimum(jnp.maximum(array, -most), most).astype(held_as)


def setup_inputs(seed: int = 0, part: int = 0) -> dict:
    seeds = jax.random.split(jax.random.key(seed), 7)
    own_keys = jax.random.split(jax.random.fold_in(seeds[6], part), 7)
    voltages = centred(own_keys[0], (INPUTS, 2, SAMPLES), 1.0, 6.0, ((0, 16),))
    taps = centred(seeds[1], (TAPS * NCH,), (TAPS * NCH) ** -0.5, 0.15625, (), jnp.float32)
    input_id = jax.random.permutation(seeds[2], INPUTS).astype(jnp.int32)
    counts = draw_counts(jax.random.fold_in(jax.random.fold_in(seeds[6], part), 71), part)
    delays = plant(jax.random.randint(own_keys[4], (BEAMS, INPUTS), 0, NCH), jax.random.fold_in(own_keys[4], 1), 0, NCH - 1).astype(jnp.int32)
    beam_owner_keys = jax.random.split(jax.random.fold_in(own_keys[5], 1), BEAMS // BEAMS_SEC)
    beam_owner_turns = jax.random.permutation(jax.random.fold_in(own_keys[5], 3), BEAMS // BEAMS_SEC)
    beam_owner = jax.vmap(lambda own, number: shared_out(jax.random.fold_in(own_keys[5], 2), own, number, BEAMS_SEC, N_CHAN, 1, MOST, 2))(beam_owner_keys, beam_owner_turns).reshape((BEAMS, 1))
    return dict(voltages=voltages, taps=taps, input_id=input_id, counts=counts, delays=delays, beam_owner=beam_owner)


def filter_table(taps):
    length = taps.shape[0]
    position = jnp.arange(length, dtype=jnp.int32) % NCH
    channel = jnp.arange(NCH, dtype=jnp.int32)
    phase = (position[:, None] * channel[None, :] % NCH).astype(jnp.float32) * (2.0 * math.pi / NCH)
    cosine = taps[:, None] * jnp.cos(phase)
    sine = taps[:, None] * jnp.sin(phase)
    upper = jnp.concatenate([cosine, -sine], axis=1)
    lower = jnp.concatenate([sine, cosine], axis=1)
    return jnp.concatenate([upper, lower], axis=0).astype(jnp.bfloat16)

def valid_mask(counts):
    position = jnp.arange(NSPEC, dtype=jnp.int32)
    return (position % SPEC < jnp.repeat(counts, SPEC)).astype(jnp.float32)

def channelize(volts, table, valid):
    count = volts.shape[0]
    frames = volts.reshape(count, 2, NSPEC + TAPS - 1, NCH).astype(jnp.float32)
    windows = jnp.concatenate([frames[:, :, k:k + NSPEC, :] for k in range(TAPS)], axis=3)
    table3 = table.astype(jnp.float32).reshape(2, TAPS * NCH, 2 * NCH)
    out = jnp.einsum('icth,chm->mit', windows, table3)
    out = out * valid[None, None, :]
    return out.reshape(2, NCH, count, NSPEC).astype(jnp.bfloat16)

def resynthesize(received, table):
    count = received.shape[0]
    table3 = table.astype(jnp.float32).reshape(2 * TAPS * NCH, 2, NCH)
    grid = jnp.einsum('pcht,mch->ptm', received.astype(jnp.float32), table3)
    grid = grid.reshape(count, NSPEC, 2, TAPS, NCH)
    total = jnp.zeros((count, NSPEC + TAPS - 1, 2, NCH), jnp.float32)
    for k in range(TAPS):
        total = total + jnp.pad(grid[:, :, :, k, :], ((0, 0), (k, TAPS - 1 - k), (0, 0), (0, 0)))
    return jnp.transpose(total, (0, 2, 1, 3)).reshape(count, 2, SAMPLES)

def reference(voltages, taps, input_id, counts, delays, beam_owner):
    table = filter_table(taps)
    valid = valid_mask(counts)
    total = jnp.sum(counts.astype(jnp.float32))
    group = math.gcd(64, INPUTS)
    grouped = voltages.reshape(INPUTS // group, group, 2, SAMPLES)
    parts = lax.map(lambda volts: channelize(volts, table, valid), grouped)
    spectra = jnp.transpose(parts, (1, 2, 0, 3, 4)).reshape(2, NCH, INPUTS, NSPEC)
    slot_of = jnp.zeros((INPUTS,), jnp.int32).at[input_id].set(jnp.arange(INPUTS, dtype=jnp.int32))
    by_id = jnp.take(spectra, slot_of, axis=2)
    per_channel = jnp.transpose(by_id, (1, 0, 2, 3))

    def correlate(data):
        first = data[0].astype(jnp.float32)
        second = data[1].astype(jnp.float32)
        real_part = jnp.dot(first, first.T) + jnp.dot(second, second.T)
        imag_part = jnp.dot(second, first.T) - jnp.dot(first, second.T)
        return (jnp.stack([real_part, imag_part]) / total).astype(jnp.bfloat16)
    visibility = lax.map(correlate, per_channel)

    def form(item):
        data, channel = item
        phase = (delays * channel % NCH).astype(jnp.float32) * (2.0 * math.pi / NCH)
        scale = 1.0 / math.sqrt(INPUTS)
        weight_cos = (jnp.cos(phase) * scale).astype(jnp.bfloat16).astype(jnp.float32)
        weight_sin = (jnp.sin(phase) * scale).astype(jnp.bfloat16).astype(jnp.float32)
        first = data[0].astype(jnp.float32)
        second = data[1].astype(jnp.float32)
        real_part = jnp.dot(weight_cos, first) - jnp.dot(weight_sin, second)
        imag_part = jnp.dot(weight_cos, second) + jnp.dot(weight_sin, first)
        return jnp.stack([real_part, imag_part]).astype(jnp.bfloat16)
    channels = jnp.arange(NCH, dtype=jnp.int32)
    beams = lax.map(form, (per_channel, channels))
    per_beam = jnp.transpose(beams, (2, 1, 0, 3))
    bunch = math.gcd(16, BEAMS)
    voices = lax.map(lambda rows: resynthesize(rows, table), per_beam.reshape(BEAMS // bunch, bunch, 2, NCH, NSPEC))
    voices = voices.reshape(BEAMS, 2, SAMPLES)
    owner = beam_owner[:, 0]
    beam = jnp.arange(BEAMS, dtype=jnp.int32)
    section = beam // BEAMS_SEC
    earlier = (section[:, None] == section[None, :]) & (owner[:, None] == owner[None, :]) & (beam[None, :] < beam[:, None])
    rank = lax.optimization_barrier(jnp.sum(earlier.astype(jnp.int32), axis=1)).astype(jnp.int32)
    slot = (owner * N_SUB + section) * MOST + rank
    resynth = jnp.zeros((SLOTS, 2, SAMPLES), jnp.float32).at[slot].set(voices)
    return (visibility, resynth)
```

```python
import functools
import math

import jax
import jax.numpy as jnp
from jax import lax
from jax.experimental import pallas as pl
from jax.experimental.pallas import tpu as pltpu
from jax.sharding import PartitionSpec as P

NCH = 128
TAPS = 12
SPEC = 8
BLOCKS = 4
BEAMS = 256


def filter_table(taps, chans):
    length = taps.shape[0]
    position = jnp.arange(length, dtype=jnp.int32) % chans
    channel = jnp.arange(chans, dtype=jnp.int32)
    phase = (position[:, None] * channel[None, :] % chans).astype(jnp.float32) * (
        2.0 * math.pi / chans
    )
    cosine = taps[:, None] * jnp.cos(phase)
    sine = taps[:, None] * jnp.sin(phase)
    upper = jnp.concatenate([cosine, -sine], axis=1)
    lower = jnp.concatenate([sine, cosine], axis=1)
    return jnp.concatenate([upper, lower], axis=0).astype(jnp.bfloat16)


def resynthesize(received, table, taps_count, chans):
    count = received.shape[0]
    spectra_n = received.shape[3]
    table3 = table.reshape(2 * taps_count * chans, 2, chans)
    grid = jnp.einsum("pcht,mch->ptm", received, table3, preferred_element_type=jnp.float32)
    grid = grid.reshape(count, spectra_n, 2, taps_count, chans)
    total = jnp.zeros((count, spectra_n + taps_count - 1, 2, chans), jnp.float32)
    for k in range(taps_count):
        total = total + jnp.pad(
            grid[:, :, :, k, :], ((0, 0), (k, taps_count - 1 - k), (0, 0), (0, 0))
        )
    return jnp.transpose(total, (0, 2, 1, 3)).reshape(
        count, 2, (spectra_n + taps_count - 1) * chans
    )


def local_plain(voltages, taps, input_id, counts, delays, beam_owner):
    n_chan = lax.axis_size("chan")
    n_sub = lax.axis_size("sub")
    inp_dev = voltages.shape[0]
    inputs = input_id.shape[0]
    chans = NCH
    taps_count = TAPS
    spectra_n = BLOCKS * SPEC
    ch_dev = chans // n_chan
    rows = inputs // n_sub
    section = BEAMS // n_sub
    most = min(section, max(2, 2 * section // n_chan))
    table = filter_table(taps, chans)
    position = jnp.arange(spectra_n, dtype=jnp.int32)
    valid = (position % SPEC < jnp.repeat(counts, SPEC)).astype(jnp.float32)
    total = jnp.sum(counts.astype(jnp.float32))
    frames = voltages.reshape(inp_dev, 2, spectra_n + taps_count - 1, chans)
    windows = jnp.concatenate(
        [frames[:, :, k : k + spectra_n, :] for k in range(taps_count)], axis=3
    )
    table3 = table.reshape(2, taps_count * chans, 2 * chans)
    filtered = jnp.einsum("icth,chm->mit", windows, table3, preferred_element_type=jnp.float32)
    filtered = filtered * valid[None, None, :]
    spectra = filtered.reshape(2, chans, inp_dev, spectra_n).astype(jnp.bfloat16)
    slot_of = jnp.zeros((inputs,), jnp.int32).at[input_id].set(jnp.arange(inputs, dtype=jnp.int32))
    turned = lax.all_to_all(spectra, "chan", split_axis=1, concat_axis=2, tiled=True)
    gathered = lax.all_gather(turned, "sub", axis=2, tiled=True)
    chan_part = slot_of // (n_sub * inp_dev)
    sub_part = slot_of // inp_dev % n_sub
    order = (sub_part * n_chan + chan_part) * inp_dev + slot_of % inp_dev
    by_id = jnp.take(gathered, order, axis=2)
    sub_index = lax.axis_index("sub")
    mine = lax.dynamic_slice_in_dim(by_id, sub_index * rows, rows, 2)
    real_part = jnp.einsum("cxit,cxjt->xij", mine, by_id, preferred_element_type=jnp.float32)
    imag_part = jnp.einsum("xit,xjt->xij", mine[1], by_id[0], preferred_element_type=jnp.float32)
    imag_part = imag_part - jnp.einsum(
        "xit,xjt->xij", mine[0], by_id[1], preferred_element_type=jnp.float32
    )
    visibility = (jnp.stack([real_part, imag_part], axis=1) / total).astype(jnp.bfloat16)
    channel = lax.axis_index("chan") * ch_dev + jnp.arange(ch_dev, dtype=jnp.int32)
    phase = (delays[None, :, :] * channel[:, None, None] % chans).astype(jnp.float32) * (
        2.0 * math.pi / chans
    )
    scale = 1.0 / math.sqrt(inputs)
    weight_cos = (jnp.cos(phase) * scale).astype(jnp.bfloat16)
    weight_sin = (jnp.sin(phase) * scale).astype(jnp.bfloat16)
    from_cos = jnp.einsum("xbi,cxit->cxbt", weight_cos, by_id, preferred_element_type=jnp.float32)
    from_sin = jnp.einsum("xbi,cxit->cxbt", weight_sin, by_id, preferred_element_type=jnp.float32)
    beams = jnp.stack([from_cos[0] - from_sin[1], from_cos[1] + from_sin[0]]).astype(jnp.bfloat16)
    owner = lax.dynamic_slice_in_dim(beam_owner[:, 0], sub_index * section, section)
    beam = jnp.arange(section, dtype=jnp.int32)
    earlier = (owner[None, :] == owner[:, None]) & (beam[None, :] < beam[:, None])
    rank = jnp.sum(earlier.astype(jnp.int32), axis=1)
    target = owner * most + rank
    select = (jnp.arange(n_chan * most, dtype=jnp.int32)[:, None] == target[None, :]).astype(
        jnp.bfloat16
    )
    placed = jnp.einsum("pb,cxbt->pcxt", select, beams, preferred_element_type=jnp.float32).astype(
        jnp.bfloat16
    )
    placed = placed.reshape(n_chan, most, 2, ch_dev, spectra_n)
    resynth = resynthesize(
        lax.all_to_all(placed, "chan", split_axis=0, concat_axis=3, tiled=True)[0],
        table,
        taps_count,
        chans,
    )
    return (visibility, resynth)


def filter_kernel(rows, pairs, steps, wide, n_chan, fr_ref, w_ref, mask_ref, out_ref):
    group = 4 if pairs % 4 == 0 else 1
    width = wide // n_chan
    for first in range(0, pairs, group):
        acc = jnp.zeros((group * rows, wide), jnp.float32)
        for k in range(steps):
            start = (first + k // 2) * rows
            acc = acc + jnp.dot(
                fr_ref[k % 2, start : start + group * rows, :],
                w_ref[k],
                preferred_element_type=jnp.float32,
            )
        for j in range(group):
            pair = first + j
            part = (acc[j * rows : (j + 1) * rows] * mask_ref[pair : pair + 1, :]).astype(
                jnp.bfloat16
            )
            for d in range(n_chan):
                out_ref[d, :, pair * width : (pair + 1) * width] = part[
                    :, d * width : (d + 1) * width
                ]


def channelize(voltages, taps, valid, n_chan):
    rows = voltages.shape[0]
    spectra_n = valid.shape[0]
    pairs = spectra_n // 2
    chans, ch_dev = NCH, NCH // n_chan
    steps = TAPS + 1
    frames_n = spectra_n + TAPS - 1
    frames = voltages.reshape(rows, 2, frames_n, chans)
    frames = jnp.transpose(frames, (2, 0, 1, 3)).reshape(frames_n, rows, 2 * chans)
    frames = jnp.pad(frames, ((0, frames_n % 2), (0, 0), (0, 0)))
    frames = frames.reshape(-1, 2, rows, 2 * chans)
    frames = jnp.transpose(frames, (1, 0, 2, 3)).reshape(2, -1, 2 * chans)
    wide = 4 * chans
    column = jnp.arange(wide, dtype=jnp.int32)
    dest, rest = column // (4 * ch_dev), column % (4 * ch_dev)
    parity, part, inner = rest // (2 * ch_dev), rest // ch_dev % 2, rest % ch_dev
    channel = dest * ch_dev + inner
    row = jnp.arange(2 * chans, dtype=jnp.int32)
    phase = (row[:, None] % chans * channel[None, :] % chans).astype(jnp.float32) * (
        2.0 * math.pi / chans
    )
    cosine, sine = jnp.cos(phase), jnp.sin(phase)
    lower = row[:, None] >= chans
    trig = jnp.where(
        lower == (part[None, :] == 1), cosine, jnp.where(lower, sine, -sine)
    )
    trig = lax.optimization_barrier(trig)
    taps2 = taps.reshape(TAPS, chans)
    taps2 = jnp.concatenate([taps2, taps2], axis=1)
    even = jnp.pad(taps2, ((0, 1), (0, 0)))
    odd = jnp.pad(taps2, ((1, 0), (0, 0)))
    factor = jnp.where(parity[None, None, :] == 0, even[:, :, None], odd[:, :, None])
    weights = (trig[None] * factor).astype(jnp.bfloat16)
    mask = jnp.where(parity[None, :] == 0, valid[0::2, None], valid[1::2, None])
    return pl.pallas_call(
        functools.partial(filter_kernel, rows, pairs, steps, wide, n_chan),
        out_shape=jax.ShapeDtypeStruct((n_chan, rows, spectra_n * 2 * ch_dev), jnp.bfloat16),
        name="filterbank",
    )(frames, weights, mask)


def turn_kernel(n_chan, n_sub, pieces, x_ref, g_ref, own_sem, zs, zr, xs, xr, cs, cr):
    me_c, me_s = lax.axis_index("chan"), lax.axis_index("sub")
    core, across = me_s % 2, me_s // 2
    n_x = n_sub // 2
    twin = me_s + 1 - 2 * core
    rows = x_ref.shape[1] // pieces
    mesh_id = pl.DeviceIdType.MESH

    def chan_of(offset):
        return (me_c + offset) % n_chan

    def sub_of(offset):
        return (across + offset) % n_x * 2 + core

    barrier = pltpu.get_barrier_semaphore()
    for j in range(1, n_chan):
        pl.semaphore_signal(barrier, device_id={"chan": chan_of(j)}, device_id_type=mesh_id)
    for j in range(1, n_x):
        pl.semaphore_signal(barrier, device_id={"sub": sub_of(j)}, device_id_type=mesh_id)
    pl.semaphore_signal(barrier, device_id={"sub": twin}, device_id_type=mesh_id)
    pl.semaphore_wait(barrier, n_chan + n_x - 1)

    def place(ref, piece):
        return ref.at[piece * rows : (piece + 1) * rows]

    def z_copy(j, h):
        return pltpu.make_async_remote_copy(
            src_ref=place(x_ref.at[chan_of(j)], h),
            dst_ref=place(g_ref.at[me_s, me_c], h),
            send_sem=zs.at[j, h],
            recv_sem=zr.at[j, h],
            device_id={"chan": chan_of(j)},
            device_id_type=mesh_id,
        )

    def source(sub, j, h):
        if j == 0:
            return place(x_ref.at[me_c], h)
        return place(g_ref.at[sub, chan_of(n_chan - j)], h)

    def x_copy(dx, j, h):
        return pltpu.make_async_remote_copy(
            src_ref=source(me_s, j, h),
            dst_ref=place(g_ref.at[me_s, chan_of(n_chan - j)], h),
            send_sem=xs.at[dx, j, h],
            recv_sem=xr.at[dx, j, h],
            device_id={"sub": sub_of(dx)},
            device_id_type=mesh_id,
        )

    def core_copy(dx, j, h):
        home = sub_of(n_x - dx)
        block = place(g_ref.at[home, chan_of(n_chan - j)], h)
        return pltpu.make_async_remote_copy(
            src_ref=source(me_s, j, h) if dx == 0 else block,
            dst_ref=block,
            send_sem=cs.at[dx, j, h],
            recv_sem=cr.at[dx, j, h],
            device_id={"sub": twin},
            device_id_type=mesh_id,
        )

    own = pltpu.make_async_copy(x_ref.at[me_c], g_ref.at[me_s, me_c], own_sem)
    started = []
    for h in range(pieces):
        for j in range(1, n_chan):
            copy = z_copy(j, h)
            copy.start()
            started.append(copy)
    own.start()

    def spread(j, h):
        for dx in range(1, n_x):
            copy = x_copy(dx, j, h)
            copy.start()
            started.append(copy)
        copy = core_copy(0, j, h)
        copy.start()
        started.append(copy)

    for h in range(pieces):
        spread(0, h)
    order = [(j, h) for h in range(pieces) for j in range(1, n_chan)]
    relay = [(j, h) for h in range(pieces) for j in range(n_chan)]
    for j, h in order:
        z_copy(j, h).wait_recv()
        spread(j, h)
    for j, h in relay:
        for dx in range(1, n_x):
            x_copy(dx, j, h).wait_recv()
            copy = core_copy(dx, j, h)
            copy.start()
            started.append(copy)
    for j, h in relay:
        for dx in range(n_x):
            core_copy(dx, j, h).wait_recv()
    for copy in started:
        copy.wait_send()
    own.wait()


def corner_turn(blocks, n_chan, n_sub):
    pieces = 2
    dma = pltpu.SemaphoreType.DMA
    n_x = n_sub // 2
    return pl.pallas_call(
        functools.partial(turn_kernel, n_chan, n_sub, pieces),
        out_shape=jax.ShapeDtypeStruct((n_sub,) + blocks.shape, jnp.bfloat16),
        in_specs=[pl.BlockSpec(memory_space=pltpu.VMEM)],
        out_specs=pl.BlockSpec(memory_space=pl.ANY),
        scratch_shapes=[
            dma,
            dma((n_chan, pieces)),
            dma((n_chan, pieces)),
            dma((n_x, n_chan, pieces)),
            dma((n_x, n_chan, pieces)),
            dma((n_x, n_chan, pieces)),
            dma((n_x, n_chan, pieces)),
        ],
        compiler_params=pltpu.CompilerParams(collective_id=0, has_side_effects=True),
        name="corner_turn",
    )(blocks)


def beam_kernel(ch_dev, spectra_n, n_chan, first_ref, g_ref, perm_ref, delay_ref, cos_ref, sin_ref, sel_ref, id_ref, out_ref, held):
    step = pl.program_id(0)

    @pl.when(step == 0)
    def _():
        wide = min(256, g_ref.shape[1])

        @pl.loop(0, g_ref.shape[1] // wide)
        def _(m):
            at = pl.multiple_of(m * wide, wide)
            sorted_part = lax.dot_general(
                g_ref[:, pl.ds(at, wide)],
                perm_ref[...],
                (((0,), (0,)), ((), ())),
                preferred_element_type=jnp.float32,
            )
            for tile in range(held.shape[0]):
                held[tile, pl.ds(at, wide), :] = sorted_part[:, tile * 128 : (tile + 1) * 128]

    def rows_of(start):
        every = pl.ds(start, spectra_n, stride=2 * ch_dev)
        return jnp.concatenate([held[tile, every, :] for tile in range(held.shape[0])], axis=1)

    both = jnp.concatenate([rows_of(step), rows_of(step + ch_dev)], axis=0).astype(jnp.bfloat16)
    id_ref[0] = both
    channel = first_ref[0] + step
    index = (delay_ref[...] * channel) & (NCH - 1)
    beams_n, inputs = index.shape
    cosine = jnp.broadcast_to(cos_ref[...], (beams_n, NCH))
    sine = jnp.broadcast_to(sin_ref[...], (beams_n, NCH))

    def look(table):
        parts = [
            jnp.take_along_axis(table, index[:, at : at + NCH], axis=1, mode="promise_in_bounds")
            for at in range(0, inputs, NCH)
        ]
        return jnp.concatenate(parts, axis=1).astype(jnp.bfloat16)

    weights = jnp.concatenate([look(cosine), look(sine)], axis=0)
    mixed = lax.dot_general(
        weights, both, (((1,), (1,)), ((), ())), preferred_element_type=jnp.float32
    )
    upper, lower = mixed[:beams_n], mixed[beams_n:]
    beam_re = upper[:, :spectra_n] - lower[:, spectra_n:]
    beam_im = upper[:, spectra_n:] + lower[:, :spectra_n]
    beams = jnp.concatenate([beam_re, beam_im], axis=1).astype(jnp.bfloat16)
    placed = jnp.dot(sel_ref[...], beams, preferred_element_type=jnp.float32).astype(jnp.bfloat16)
    out_ref[:, 0] = placed.reshape(n_chan, placed.shape[0] // n_chan, placed.shape[1])


def form_beams(gathered, perm, delays, tables, select, first, ch_dev, spectra_n, n_chan):
    inputs = perm.shape[0]
    slots, beams_n = select.shape
    whole = lambda shape: pl.BlockSpec(shape, lambda f, s: (0,) * len(shape), pipeline_mode=pl.Buffered(1))
    cols = gathered.shape[1]
    return pl.pallas_call(
        functools.partial(beam_kernel, ch_dev, spectra_n, n_chan),
        grid_spec=pltpu.PrefetchScalarGridSpec(
            num_scalar_prefetch=1,
            grid=(ch_dev,),
            in_specs=[
                whole((inputs, cols)),
                whole((inputs, inputs)),
                whole((beams_n, inputs)),
                whole((1, NCH)),
                whole((1, NCH)),
                whole((slots, beams_n)),
            ],
            out_specs=[
                pl.BlockSpec((1, 2 * spectra_n, inputs), lambda f, s: (f, 0, 0)),
                pl.BlockSpec((n_chan, 1, slots // n_chan, 2 * spectra_n), lambda f, s: (0, f, 0, 0)),
            ],
            scratch_shapes=[pltpu.VMEM((inputs // 128, cols, 128), jnp.float32)],
        ),
        out_shape=[
            jax.ShapeDtypeStruct((ch_dev, 2 * spectra_n, inputs), jnp.bfloat16),
            jax.ShapeDtypeStruct((n_chan, ch_dev, slots // n_chan, 2 * spectra_n), jnp.bfloat16),
        ],
        compiler_params=pltpu.CompilerParams(dimension_semantics=("arbitrary",)),
        name="beams",
    )(first, gathered, perm, delays, *tables, select)


def visibility_kernel(sub_ref, scale_ref, left_ref, right_ref, out_ref):
    for j in range(left_ref.shape[0]):
        left = left_ref[j]
        half, rows = left.shape[0] // 2, left.shape[1]
        turned = jnp.concatenate([left[half:], -left[:half]], axis=0)
        both = jnp.concatenate([left, turned], axis=1)
        product = lax.dot_general(
            both, right_ref[j], (((0,), (0,)), ((), ())), preferred_element_type=jnp.float32
        )
        product = (product * scale_ref[0]).astype(jnp.bfloat16)
        out_ref[j, 0] = product[:rows]
        out_ref[j, 1] = product[rows:]


def correlate(by_id, scale, sub_index, rows):
    ch_dev, depth, inputs = by_id.shape
    group = 2 if ch_dev % 2 == 0 else 1
    return pl.pallas_call(
        visibility_kernel,
        grid_spec=pltpu.PrefetchScalarGridSpec(
            num_scalar_prefetch=1,
            grid=(ch_dev // group,),
            in_specs=[
                pl.BlockSpec(memory_space=pltpu.SMEM),
                pl.BlockSpec((group, depth, rows), lambda f, s: (f, 0, s[0])),
                pl.BlockSpec((group, depth, inputs), lambda f, s: (f, 0, 0)),
            ],
            out_specs=pl.BlockSpec((group, 2, rows, inputs), lambda f, s: (f, 0, 0, 0)),
        ),
        out_shape=jax.ShapeDtypeStruct((ch_dev, 2, rows, inputs), jnp.bfloat16),
        cost_estimate=pl.CostEstimate(
            flops=4 * ch_dev * rows * inputs * depth,
            bytes_accessed=4 * ch_dev * rows * inputs,
            transcendentals=0,
        ),
        name="visibility",
    )(sub_index, scale, by_id, by_id)


def voice_kernel(spectra_n, count, frames_n, b_ref, w_ref, out_ref):
    chans = w_ref.shape[2] // 2
    group = 4
    for first in range(0, frames_n, group):
        size = min(group, frames_n - first)
        acc = jnp.zeros((size * count, w_ref.shape[2]), jnp.float32)
        for k in range(TAPS):
            low = first - k
            if low + size <= 0 or low >= spectra_n:
                continue
            start = (low + TAPS - 1) * count
            acc = acc + jnp.dot(
                b_ref[start : start + size * count, :], w_ref[k], preferred_element_type=jnp.float32
            )
        for j in range(size):
            at = (first + j) * chans
            for c in range(2):
                out_ref[c, :, at : at + chans] = acc[
                    j * count : (j + 1) * count, c * chans : (c + 1) * chans
                ]


def synthesize(received, taps):
    chans, count, _ = received.shape
    spectra_n = received.shape[2] // 2
    frames_n = spectra_n + TAPS - 1
    bank = received.reshape(chans, count, 2, spectra_n)
    bank = jnp.transpose(bank, (3, 1, 2, 0)).reshape(spectra_n, count, 2 * chans)
    bank = jnp.pad(bank, ((TAPS - 1, TAPS - 1), (0, 0), (0, 0))).reshape(-1, 2 * chans)
    index = jnp.arange(2 * chans, dtype=jnp.int32)
    inner = index % chans
    phase = (inner[:, None] * inner[None, :] % chans).astype(jnp.float32) * (2.0 * math.pi / chans)
    cosine, sine = jnp.cos(phase), jnp.sin(phase)
    from_im, to_im = index[:, None] >= chans, index[None, :] >= chans
    trig = jnp.where(from_im == to_im, cosine, jnp.where(to_im, sine, -sine))
    trig = lax.optimization_barrier(trig)
    taps2 = taps.reshape(TAPS, 1, chans)
    weights = (trig[None] * jnp.concatenate([taps2, taps2], axis=2)).astype(jnp.bfloat16)
    voices = pl.pallas_call(
        functools.partial(voice_kernel, spectra_n, count, frames_n),
        out_shape=jax.ShapeDtypeStruct((2, count, frames_n * chans), jnp.float32),
        name="voices",
    )(bank, weights)
    return jnp.transpose(voices, (1, 0, 2))


def local(voltages, taps, input_id, counts, delays, beam_owner):
    n_chan = lax.axis_size("chan")
    n_sub = lax.axis_size("sub")
    inp_dev = voltages.shape[0]
    inputs = input_id.shape[0]
    chans = NCH
    spectra_n = BLOCKS * SPEC
    ch_dev = chans // n_chan
    rows = inputs // n_sub
    section = BEAMS // n_sub
    most = min(section, max(2, 2 * section // n_chan))
    if inp_dev % 32 or 4 * ch_dev % 128 or rows % 128 or n_sub % 2 or most % 16:
        return local_plain(voltages, taps, input_id, counts, delays, beam_owner)
    position = jnp.arange(spectra_n, dtype=jnp.int32)
    valid = (position % SPEC < jnp.repeat(counts, SPEC)).astype(jnp.float32)
    total = jnp.sum(counts.astype(jnp.float32))
    chan_index, sub_index = lax.axis_index("chan"), lax.axis_index("sub")
    blocks = channelize(voltages, taps, valid, n_chan)
    gathered = corner_turn(blocks, n_chan, n_sub).reshape(inputs, -1)
    names = jnp.transpose(input_id.reshape(n_chan, n_sub, inp_dev), (1, 0, 2)).reshape(inputs)
    perm = (names[:, None] == jnp.arange(inputs, dtype=jnp.int32)[None, :]).astype(jnp.bfloat16)
    angle = jnp.arange(chans, dtype=jnp.int32).astype(jnp.float32) * (2.0 * math.pi / chans)
    scale = 1.0 / math.sqrt(inputs)
    tables = [
        (wave(angle) * scale).astype(jnp.bfloat16).astype(jnp.float32)[None, :]
        for wave in (jnp.cos, jnp.sin)
    ]
    owner = lax.dynamic_slice_in_dim(beam_owner[:, 0], sub_index * section, section)
    beam = jnp.arange(section, dtype=jnp.int32)
    earlier = (owner[None, :] == owner[:, None]) & (beam[None, :] < beam[:, None])
    rank = jnp.sum(earlier.astype(jnp.int32), axis=1)
    target = owner * most + rank
    select = (jnp.arange(n_chan * most, dtype=jnp.int32)[:, None] == target[None, :]).astype(
        jnp.bfloat16
    )
    by_id, placed = form_beams(
        gathered,
        perm,
        delays,
        tables,
        select,
        (chan_index * ch_dev).astype(jnp.int32)[None],
        ch_dev,
        spectra_n,
        n_chan,
    )
    received = lax.all_to_all(placed, "chan", split_axis=0, concat_axis=0, tiled=True)
    visibility = correlate(by_id, (1.0 / total)[None], sub_index.astype(jnp.int32)[None], rows)
    resynth = synthesize(received.reshape(chans, most, 2 * spectra_n), taps)
    return (visibility, resynth)


def solution(mesh):
    placed = (
        P(("grp", "chan", "sub"), None, None),
        P(),
        P(),
        P("grp"),
        P(("grp", "sub"), None),
        P("grp", None),
    )
    return jax.shard_map(
        local,
        mesh=mesh,
        in_specs=placed,
        out_specs=(P(("grp", "chan"), None, "sub", None), P(("grp", "chan", "sub"), None, None)),
        check_vma=False,
    )
```

```python
import functools
import math

import jax
import jax.numpy as jnp
from jax import lax
from jax.experimental import pallas as pl
from jax.experimental.pallas import tpu as pltpu
from jax.sharding import PartitionSpec as P

NCH = 128
TAPS = 12
SPEC = 8
BLOCKS = 4
BEAMS = 256


def filter_table(taps, chans):
    length = taps.shape[0]
    position = jnp.arange(length, dtype=jnp.int32) % chans
    channel = jnp.arange(chans, dtype=jnp.int32)
    phase = (position[:, None] * channel[None, :] % chans).astype(jnp.float32) * (
        2.0 * math.pi / chans
    )
    cosine = taps[:, None] * jnp.cos(phase)
    sine = taps[:, None] * jnp.sin(phase)
    upper = jnp.concatenate([cosine, -sine], axis=1)
    lower = jnp.concatenate([sine, cosine], axis=1)
    return jnp.concatenate([upper, lower], axis=0).astype(jnp.bfloat16)


def resynthesize(received, table, taps_count, chans):
    count = received.shape[0]
    spectra_n = received.shape[3]
    table3 = table.reshape(2 * taps_count * chans, 2, chans)
    grid = jnp.einsum("pcht,mch->ptm", received, table3, preferred_element_type=jnp.float32)
    grid = grid.reshape(count, spectra_n, 2, taps_count, chans)
    total = jnp.zeros((count, spectra_n + taps_count - 1, 2, chans), jnp.float32)
    for k in range(taps_count):
        total = total + jnp.pad(
            grid[:, :, :, k, :], ((0, 0), (k, taps_count - 1 - k), (0, 0), (0, 0))
        )
    return jnp.transpose(total, (0, 2, 1, 3)).reshape(
        count, 2, (spectra_n + taps_count - 1) * chans
    )


def local_plain(voltages, taps, input_id, counts, delays, beam_owner):
    n_chan = lax.axis_size("chan")
    n_sub = lax.axis_size("sub")
    inp_dev = voltages.shape[0]
    inputs = input_id.shape[0]
    chans = NCH
    taps_count = TAPS
    spectra_n = BLOCKS * SPEC
    ch_dev = chans // n_chan
    rows = inputs // n_sub
    section = BEAMS // n_sub
    most = min(section, max(2, 2 * section // n_chan))
    table = filter_table(taps, chans)
    position = jnp.arange(spectra_n, dtype=jnp.int32)
    valid = (position % SPEC < jnp.repeat(counts, SPEC)).astype(jnp.float32)
    total = jnp.sum(counts.astype(jnp.float32))
    frames = voltages.reshape(inp_dev, 2, spectra_n + taps_count - 1, chans)
    windows = jnp.concatenate(
        [frames[:, :, k : k + spectra_n, :] for k in range(taps_count)], axis=3
    )
    table3 = table.reshape(2, taps_count * chans, 2 * chans)
    filtered = jnp.einsum("icth,chm->mit", windows, table3, preferred_element_type=jnp.float32)
    filtered = filtered * valid[None, None, :]
    spectra = filtered.reshape(2, chans, inp_dev, spectra_n).astype(jnp.bfloat16)
    slot_of = jnp.zeros((inputs,), jnp.int32).at[input_id].set(jnp.arange(inputs, dtype=jnp.int32))
    turned = lax.all_to_all(spectra, "chan", split_axis=1, concat_axis=2, tiled=True)
    gathered = lax.all_gather(turned, "sub", axis=2, tiled=True)
    chan_part = slot_of // (n_sub * inp_dev)
    sub_part = slot_of // inp_dev % n_sub
    order = (sub_part * n_chan + chan_part) * inp_dev + slot_of % inp_dev
    by_id = jnp.take(gathered, order, axis=2)
    sub_index = lax.axis_index("sub")
    mine = lax.dynamic_slice_in_dim(by_id, sub_index * rows, rows, 2)
    real_part = jnp.einsum("cxit,cxjt->xij", mine, by_id, preferred_element_type=jnp.float32)
    imag_part = jnp.einsum("xit,xjt->xij", mine[1], by_id[0], preferred_element_type=jnp.float32)
    imag_part = imag_part - jnp.einsum(
        "xit,xjt->xij", mine[0], by_id[1], preferred_element_type=jnp.float32
    )
    visibility = (jnp.stack([real_part, imag_part], axis=1) / total).astype(jnp.bfloat16)
    channel = lax.axis_index("chan") * ch_dev + jnp.arange(ch_dev, dtype=jnp.int32)
    phase = (delays[None, :, :] * channel[:, None, None] % chans).astype(jnp.float32) * (
        2.0 * math.pi / chans
    )
    scale = 1.0 / math.sqrt(inputs)
    weight_cos = (jnp.cos(phase) * scale).astype(jnp.bfloat16)
    weight_sin = (jnp.sin(phase) * scale).astype(jnp.bfloat16)
    from_cos = jnp.einsum("xbi,cxit->cxbt", weight_cos, by_id, preferred_element_type=jnp.float32)
    from_sin = jnp.einsum("xbi,cxit->cxbt", weight_sin, by_id, preferred_element_type=jnp.float32)
    beams = jnp.stack([from_cos[0] - from_sin[1], from_cos[1] + from_sin[0]]).astype(jnp.bfloat16)
    owner = lax.dynamic_slice_in_dim(beam_owner[:, 0], sub_index * section, section)
    beam = jnp.arange(section, dtype=jnp.int32)
    earlier = (owner[None, :] == owner[:, None]) & (beam[None, :] < beam[:, None])
    rank = jnp.sum(earlier.astype(jnp.int32), axis=1)
    target = owner * most + rank
    select = (jnp.arange(n_chan * most, dtype=jnp.int32)[:, None] == target[None, :]).astype(
        jnp.bfloat16
    )
    placed = jnp.einsum("pb,cxbt->pcxt", select, beams, preferred_element_type=jnp.float32).astype(
        jnp.bfloat16
    )
    placed = placed.reshape(n_chan, most, 2, ch_dev, spectra_n)
    resynth = resynthesize(
        lax.all_to_all(placed, "chan", split_axis=0, concat_axis=3, tiled=True)[0],
        table,
        taps_count,
        chans,
    )
    return (visibility, resynth)


def filter_kernel(rows, pairs, steps, wide, n_chan, fr_ref, w_ref, mask_ref, out_ref):
    group = 4 if pairs % 4 == 0 else 1
    width = wide // n_chan
    for first in range(0, pairs, group):
        acc = jnp.zeros((group * rows, wide), jnp.float32)
        for k in range(steps):
            window = jnp.concatenate(
                [
                    jnp.concatenate([fr_ref[0, at], fr_ref[1, at]], axis=1)
                    for at in range(2 * first + k, 2 * (first + group) + k, 2)
                ],
                axis=0,
            )
            acc = acc + jnp.dot(window, w_ref[k], preferred_element_type=jnp.float32)
        for j in range(group):
            pair = first + j
            part = (acc[j * rows : (j + 1) * rows] * mask_ref[pair : pair + 1, :]).astype(
                jnp.bfloat16
            )
            for d in range(n_chan):
                out_ref[d, :, pair * width : (pair + 1) * width] = part[
                    :, d * width : (d + 1) * width
                ]


def channelize(voltages, taps, valid, n_chan):
    rows = voltages.shape[0]
    spectra_n = valid.shape[0]
    pairs = spectra_n // 2
    chans, ch_dev = NCH, NCH // n_chan
    steps = TAPS + 1
    frames_n = spectra_n + TAPS - 1
    frames = voltages.reshape(rows, 2, frames_n, chans)
    frames = jnp.transpose(frames, (1, 2, 0, 3))
    wide = 4 * chans
    column = jnp.arange(wide, dtype=jnp.int32)
    dest, rest = column // (4 * ch_dev), column % (4 * ch_dev)
    parity, part, inner = rest // (2 * ch_dev), rest // ch_dev % 2, rest % ch_dev
    channel = dest * ch_dev + inner
    row = jnp.arange(2 * chans, dtype=jnp.int32)
    phase = (row[:, None] % chans * channel[None, :] % chans).astype(jnp.float32) * (
        2.0 * math.pi / chans
    )
    cosine, sine = jnp.cos(phase), jnp.sin(phase)
    lower = row[:, None] >= chans
    trig = jnp.where(
        lower == (part[None, :] == 1), cosine, jnp.where(lower, sine, -sine)
    )
    trig = lax.optimization_barrier(trig)
    taps2 = taps.reshape(TAPS, chans)
    taps2 = jnp.concatenate([taps2, taps2], axis=1)
    even = jnp.pad(taps2, ((0, 1), (0, 0)))
    odd = jnp.pad(taps2, ((1, 0), (0, 0)))
    factor = jnp.where(parity[None, None, :] == 0, even[:, :, None], odd[:, :, None])
    weights = (trig[None] * factor).astype(jnp.bfloat16)
    mask = jnp.where(parity[None, :] == 0, valid[0::2, None], valid[1::2, None])
    return pl.pallas_call(
        functools.partial(filter_kernel, rows, pairs, steps, wide, n_chan),
        out_shape=jax.ShapeDtypeStruct((n_chan, rows, spectra_n * 2 * ch_dev), jnp.bfloat16),
        name="filterbank",
    )(frames, weights, mask)


def weigh(channel, scale, delay_ref, out_ref, f):
    beams_n, inputs = delay_ref.shape
    high, wide = 16, 512
    unit = 2.0 * math.pi / NCH
    quarter = NCH // 4

    @pl.loop(0, beams_n // high)
    def _(row):
        at = pl.multiple_of(row * high, high)
        for left in range(0, inputs, wide):
            turn = (delay_ref[pl.ds(at, high), left : left + wide] * channel) & (NCH - 1)
            quadrant = (turn + quarter // 2) >> (quarter.bit_length() - 1)
            x = (turn - quadrant * quarter).astype(jnp.float32) * unit
            y = x * x
            even = 1.0 + y * (-1 / 2 + y * (1 / 24 + y * (-1 / 720 + y * (1 / 40320))))
            odd = x * (1.0 + y * (-1 / 6 + y * (1 / 120 + y * (-1 / 5040 + y * (1 / 362880)))))
            swap = (quadrant & 1) == 1
            cosine = jnp.where(swap, odd, even) * scale
            sine = jnp.where(swap, even, odd) * scale
            cosine = jnp.where(((quadrant + 1) & 2) == 2, -cosine, cosine)
            sine = jnp.where((quadrant & 2) == 2, -sine, sine)
            out_ref[f, pl.ds(at, high), left : left + wide] = cosine.astype(jnp.bfloat16)
            low = pl.multiple_of(at + beams_n, high)
            out_ref[f, pl.ds(low, high), left : left + wide] = sine.astype(jnp.bfloat16)


def turn_kernel(n_chan, n_sub, pieces, scale, x_ref, delay_ref, g_ref, weight_ref, own_sem, zs, zr, xs, xr, cs, cr):
    me_c, me_s = lax.axis_index("chan"), lax.axis_index("sub")
    core, across = me_s % 2, me_s // 2
    n_x = n_sub // 2
    twin = me_s + 1 - 2 * core
    rows = x_ref.shape[1] // pieces
    mesh_id = pl.DeviceIdType.MESH

    def chan_of(offset):
        return (me_c + offset) % n_chan

    def sub_of(offset):
        return (across + offset) % n_x * 2 + core

    barrier = pltpu.get_barrier_semaphore()
    for j in range(1, n_chan):
        pl.semaphore_signal(barrier, device_id={"chan": chan_of(j)}, device_id_type=mesh_id)
    for j in range(1, n_x):
        pl.semaphore_signal(barrier, device_id={"sub": sub_of(j)}, device_id_type=mesh_id)
    pl.semaphore_signal(barrier, device_id={"sub": twin}, device_id_type=mesh_id)
    pl.semaphore_wait(barrier, n_chan + n_x - 1)

    def place(ref, piece):
        return ref.at[piece * rows : (piece + 1) * rows]

    def z_copy(j, h):
        return pltpu.make_async_remote_copy(
            src_ref=place(x_ref.at[chan_of(j)], h),
            dst_ref=place(g_ref.at[me_s, me_c], h),
            send_sem=zs.at[j, h],
            recv_sem=zr.at[j, h],
            device_id={"chan": chan_of(j)},
            device_id_type=mesh_id,
        )

    def source(sub, j, h):
        if j == 0:
            return place(x_ref.at[me_c], h)
        return place(g_ref.at[sub, chan_of(n_chan - j)], h)

    def x_copy(dx, j, h):
        return pltpu.make_async_remote_copy(
            src_ref=source(me_s, j, h),
            dst_ref=place(g_ref.at[me_s, chan_of(n_chan - j)], h),
            send_sem=xs.at[dx, j, h],
            recv_sem=xr.at[dx, j, h],
            device_id={"sub": sub_of(dx)},
            device_id_type=mesh_id,
        )

    def core_copy(dx, j, h):
        home = sub_of(n_x - dx)
        block = place(g_ref.at[home, chan_of(n_chan - j)], h)
        return pltpu.make_async_remote_copy(
            src_ref=source(me_s, j, h) if dx == 0 else block,
            dst_ref=block,
            send_sem=cs.at[dx, j, h],
            recv_sem=cr.at[dx, j, h],
            device_id={"sub": twin},
            device_id_type=mesh_id,
        )

    own = pltpu.make_async_copy(x_ref.at[me_c], g_ref.at[me_s, me_c], own_sem)
    started = []
    for h in range(pieces):
        for j in range(1, n_chan):
            copy = z_copy(j, h)
            copy.start()
            started.append(copy)
    own.start()

    def spread(j, h):
        for dx in range(1, n_x):
            copy = x_copy(dx, j, h)
            copy.start()
            started.append(copy)
        copy = core_copy(0, j, h)
        copy.start()
        started.append(copy)

    for h in range(pieces):
        spread(0, h)
    ch_dev = weight_ref.shape[0]
    slots = pieces * (2 * n_chan - 1)
    share = -(-ch_dev * 4 // (3 * slots))
    done = [0]

    def work():
        first, last = done[0], min(ch_dev, done[0] + share)
        done[0] = last
        if first < last:

            @pl.loop(first, last)
            def _(f):
                weigh(me_c * ch_dev + f, scale, delay_ref, weight_ref, f)

    def relay(h):
        for j in range(n_chan):
            work()
            for dx in range(1, n_x):
                x_copy(dx, j, h).wait_recv()
                copy = core_copy(dx, j, h)
                copy.start()
                started.append(copy)

    for h in range(pieces):
        for j in range(1, n_chan):
            work()
            z_copy(j, h).wait_recv()
            spread(j, h)
        if h > 0:
            relay(h - 1)
    relay(pieces - 1)
    while done[0] < ch_dev:
        work()
    for h in range(pieces):
        for j in range(n_chan):
            for dx in range(n_x):
                core_copy(dx, j, h).wait_recv()
    for copy in started:
        copy.wait_send()
    own.wait()


def corner_turn(blocks, delays, n_chan, n_sub):
    pieces = 4
    dma = pltpu.SemaphoreType.DMA
    n_x = n_sub // 2
    beams_n, inputs = delays.shape
    return pl.pallas_call(
        functools.partial(turn_kernel, n_chan, n_sub, pieces, 1.0 / math.sqrt(inputs)),
        out_shape=[
            jax.ShapeDtypeStruct((n_sub,) + blocks.shape, jnp.bfloat16),
            jax.ShapeDtypeStruct((NCH // n_chan, 2 * beams_n, inputs), jnp.bfloat16),
        ],
        in_specs=[pl.BlockSpec(memory_space=pltpu.VMEM)] * 2,
        out_specs=[pl.BlockSpec(memory_space=pl.ANY), pl.BlockSpec(memory_space=pltpu.VMEM)],
        scratch_shapes=[
            dma,
            dma((n_chan, pieces)),
            dma((n_chan, pieces)),
            dma((n_x, n_chan, pieces)),
            dma((n_x, n_chan, pieces)),
            dma((n_x, n_chan, pieces)),
            dma((n_x, n_chan, pieces)),
        ],
        compiler_params=pltpu.CompilerParams(collective_id=0, has_side_effects=True),
        name="corner_turn",
    )(blocks, delays)


def beam_kernel(ch_dev, spectra_n, n_chan, batch, g_ref, perm_ref, weight_ref, sel_ref, id_ref, out_ref, held, ready, own_sem, send, recv):
    step = pl.program_id(0)
    pair = weight_ref.shape[0]
    steps = ch_dev // pair
    me_c = lax.axis_index("chan")
    mesh_id = pl.DeviceIdType.MESH

    @pl.when(step == 0)
    def _():
        barrier = pltpu.get_barrier_semaphore()
        for j in range(1, n_chan):
            pl.semaphore_signal(
                barrier, device_id={"chan": (me_c + j) % n_chan}, device_id_type=mesh_id
            )
        wide = min(256, g_ref.shape[1])

        @pl.loop(0, g_ref.shape[1] // wide)
        def _(m):
            at = pl.multiple_of(m * wide, wide)
            sorted_part = lax.dot_general(
                g_ref[:, pl.ds(at, wide)],
                perm_ref[...],
                (((0,), (0,)), ((), ())),
                preferred_element_type=jnp.float32,
            )
            for tile in range(held.shape[0]):
                held[tile, pl.ds(at, wide), :] = sorted_part[:, tile * 128 : (tile + 1) * 128]

        pl.semaphore_wait(barrier, n_chan - 1)

    def rows_of(start):
        every = pl.ds(start, spectra_n, stride=2 * ch_dev)
        return jnp.concatenate([held[tile, every, :] for tile in range(held.shape[0])], axis=1)

    def form(j):
        f = step * pair + j
        both = jnp.concatenate([rows_of(f), rows_of(f + ch_dev)], axis=0).astype(jnp.bfloat16)
        id_ref[j] = both
        mixed = lax.dot_general(
            weight_ref[j], both, (((1,), (1,)), ((), ())), preferred_element_type=jnp.float32
        )
        beams_n = mixed.shape[0] // 2
        upper, lower = mixed[:beams_n], mixed[beams_n:]
        beam_re = upper[:, :spectra_n] - lower[:, spectra_n:]
        beam_im = upper[:, spectra_n:] + lower[:, :spectra_n]
        return [beam_re, beam_im]

    beams = jnp.concatenate(form(0) + form(1), axis=1).astype(jnp.bfloat16)
    placed = jnp.dot(sel_ref[...], beams, preferred_element_type=jnp.float32).astype(jnp.bfloat16)
    most = placed.shape[0] // n_chan
    for d in range(n_chan):
        ready[d, step] = placed[d * most : (d + 1) * most]

    def copy_of(b, j):
        to = (me_c + j) % n_chan
        return pltpu.make_async_remote_copy(
            src_ref=ready.at[to, pl.ds(b * batch, batch)],
            dst_ref=out_ref.at[me_c, pl.ds(b * batch, batch)],
            send_sem=send.at[b, j],
            recv_sem=recv.at[b, j],
            device_id={"chan": to},
            device_id_type=mesh_id,
        )

    for b in range(steps // batch):

        @pl.when(step == (b + 1) * batch - 1)
        def _():
            for j in range(1, n_chan):
                copy_of(b, j).start()

    @pl.when(step == steps - 1)
    def _():
        own = pltpu.make_async_copy(ready.at[me_c], out_ref.at[me_c], own_sem)
        own.start()
        for b in range(steps // batch):
            for j in range(1, n_chan):
                copy_of(b, j).wait_recv()
        for b in range(steps // batch):
            for j in range(1, n_chan):
                copy_of(b, j).wait_send()
        own.wait()


def form_beams(gathered, perm, weights, select, spectra_n, n_chan):
    inputs = perm.shape[0]
    ch_dev, double_n, _ = weights.shape
    slots, beams_n = select.shape
    cols = gathered.shape[1]
    pair = 2
    steps = ch_dev // pair
    batch = steps // 4
    dma = pltpu.SemaphoreType.DMA
    whole = lambda shape: pl.BlockSpec(
        shape, lambda f: (0,) * len(shape), pipeline_mode=pl.Buffered(1)
    )
    travel = (n_chan, steps, slots // n_chan, 2 * pair * spectra_n)
    return pl.pallas_call(
        functools.partial(beam_kernel, ch_dev, spectra_n, n_chan, batch),
        grid=(steps,),
        in_specs=[
            whole((inputs, cols)),
            whole((inputs, inputs)),
            pl.BlockSpec((pair, double_n, inputs), lambda f: (f, 0, 0)),
            whole((slots, beams_n)),
        ],
        out_specs=[
            pl.BlockSpec((pair, 2 * spectra_n, inputs), lambda f: (f, 0, 0)),
            pl.BlockSpec(memory_space=pl.ANY),
        ],
        scratch_shapes=[
            pltpu.VMEM((inputs // 128, cols, 128), jnp.float32),
            pltpu.VMEM(travel, jnp.bfloat16),
            dma,
            dma((4, n_chan)),
            dma((4, n_chan)),
        ],
        out_shape=[
            jax.ShapeDtypeStruct((ch_dev, 2 * spectra_n, inputs), jnp.bfloat16),
            jax.ShapeDtypeStruct(travel, jnp.bfloat16),
        ],
        compiler_params=pltpu.CompilerParams(
            dimension_semantics=("arbitrary",), collective_id=1, has_side_effects=True
        ),
        name="beams",
    )(gathered, perm, weights, select)


def visibility_kernel(sub_ref, scale_ref, left_ref, right_ref, out_ref):
    for j in range(left_ref.shape[0]):
        left = left_ref[j]
        half, rows = left.shape[0] // 2, left.shape[1]
        turned = jnp.concatenate([left[half:], -left[:half]], axis=0)
        both = jnp.concatenate([left, turned], axis=1)
        product = lax.dot_general(
            both, right_ref[j], (((0,), (0,)), ((), ())), preferred_element_type=jnp.float32
        )
        product = (product * scale_ref[0]).astype(jnp.bfloat16)
        out_ref[j, 0] = product[:rows]
        out_ref[j, 1] = product[rows:]


def correlate(by_id, scale, sub_index, rows):
    ch_dev, depth, inputs = by_id.shape
    group = 2 if ch_dev % 2 == 0 else 1
    return pl.pallas_call(
        visibility_kernel,
        grid_spec=pltpu.PrefetchScalarGridSpec(
            num_scalar_prefetch=1,
            grid=(ch_dev // group,),
            in_specs=[
                pl.BlockSpec(memory_space=pltpu.SMEM),
                pl.BlockSpec((group, depth, rows), lambda f, s: (f, 0, s[0])),
                pl.BlockSpec((group, depth, inputs), lambda f, s: (f, 0, 0)),
            ],
            out_specs=pl.BlockSpec((group, 2, rows, inputs), lambda f, s: (f, 0, 0, 0)),
        ),
        out_shape=jax.ShapeDtypeStruct((ch_dev, 2, rows, inputs), jnp.bfloat16),
        cost_estimate=pl.CostEstimate(
            flops=4 * ch_dev * rows * inputs * depth,
            bytes_accessed=4 * ch_dev * rows * inputs,
            transcendentals=0,
        ),
        name="visibility",
    )(sub_index, scale, by_id, by_id)


def voice_kernel(spectra_n, count, frames_n, b_ref, w_ref, out_ref):
    chans = w_ref.shape[2] // 2
    group = 4
    for first in range(0, frames_n, group):
        size = min(group, frames_n - first)
        acc = jnp.zeros((size * count, w_ref.shape[2]), jnp.float32)
        for k in range(TAPS):
            low = first - k
            if low + size <= 0 or low >= spectra_n:
                continue
            start = (low + TAPS - 1) * count
            acc = acc + jnp.dot(
                b_ref[start : start + size * count, :], w_ref[k], preferred_element_type=jnp.float32
            )
        for j in range(size):
            at = (first + j) * chans
            for c in range(2):
                out_ref[:, c, at : at + chans] = acc[
                    j * count : (j + 1) * count, c * chans : (c + 1) * chans
                ]


def synthesize(received, taps):
    n_chan, steps, count, width = received.shape
    spectra_n = BLOCKS * SPEC
    pair = width // (2 * spectra_n)
    chans = n_chan * steps * pair
    frames_n = spectra_n + TAPS - 1
    bank = received.reshape(n_chan * steps, count, pair, 2, spectra_n)
    bank = jnp.transpose(bank, (4, 1, 3, 0, 2)).reshape(spectra_n, count, 2 * chans)
    bank = jnp.pad(bank, ((TAPS - 1, TAPS - 1), (0, 0), (0, 0))).reshape(-1, 2 * chans)
    index = jnp.arange(2 * chans, dtype=jnp.int32)
    inner = index % chans
    phase = (inner[:, None] * inner[None, :] % chans).astype(jnp.float32) * (2.0 * math.pi / chans)
    cosine, sine = jnp.cos(phase), jnp.sin(phase)
    from_im, to_im = index[:, None] >= chans, index[None, :] >= chans
    trig = jnp.where(from_im == to_im, cosine, jnp.where(to_im, sine, -sine))
    trig = lax.optimization_barrier(trig)
    taps2 = taps.reshape(TAPS, 1, chans)
    weights = (trig[None] * jnp.concatenate([taps2, taps2], axis=2)).astype(jnp.bfloat16)
    return pl.pallas_call(
        functools.partial(voice_kernel, spectra_n, count, frames_n),
        out_shape=jax.ShapeDtypeStruct((count, 2, frames_n * chans), jnp.float32),
        name="voices",
    )(bank, weights)


def local(voltages, taps, input_id, counts, delays, beam_owner):
    n_chan = lax.axis_size("chan")
    n_sub = lax.axis_size("sub")
    inp_dev = voltages.shape[0]
    inputs = input_id.shape[0]
    chans = NCH
    spectra_n = BLOCKS * SPEC
    ch_dev = chans // n_chan
    rows = inputs // n_sub
    section = BEAMS // n_sub
    most = min(section, max(2, 2 * section // n_chan))
    if inp_dev % 32 or 4 * ch_dev % 128 or rows % 128 or n_sub % 2 or most % 16:
        return local_plain(voltages, taps, input_id, counts, delays, beam_owner)
    position = jnp.arange(spectra_n, dtype=jnp.int32)
    valid = (position % SPEC < jnp.repeat(counts, SPEC)).astype(jnp.float32)
    total = jnp.sum(counts.astype(jnp.float32))
    sub_index = lax.axis_index("sub")
    blocks = channelize(voltages, taps, valid, n_chan)
    gathered, weights = corner_turn(blocks, delays, n_chan, n_sub)
    gathered = gathered.reshape(inputs, -1)
    names = jnp.transpose(input_id.reshape(n_chan, n_sub, inp_dev), (1, 0, 2)).reshape(inputs)
    perm = (names[:, None] == jnp.arange(inputs, dtype=jnp.int32)[None, :]).astype(jnp.bfloat16)
    owner = lax.dynamic_slice_in_dim(beam_owner[:, 0], sub_index * section, section)
    beam = jnp.arange(section, dtype=jnp.int32)
    earlier = (owner[None, :] == owner[:, None]) & (beam[None, :] < beam[:, None])
    rank = jnp.sum(earlier.astype(jnp.int32), axis=1)
    target = owner * most + rank
    select = (jnp.arange(n_chan * most, dtype=jnp.int32)[:, None] == target[None, :]).astype(
        jnp.bfloat16
    )
    by_id, received = form_beams(gathered, perm, weights, select, spectra_n, n_chan)
    visibility = correlate(by_id, (1.0 / total)[None], sub_index.astype(jnp.int32)[None], rows)
    resynth = synthesize(received, taps)
    return (visibility, resynth)


def solution(mesh):
    placed = (
        P(("grp", "chan", "sub"), None, None),
        P(),
        P(),
        P("grp"),
        P(("grp", "sub"), None),
        P("grp", None),
    )
    return jax.shard_map(
        local,
        mesh=mesh,
        in_specs=placed,
        out_specs=(P(("grp", "chan"), None, "sub", None), P(("grp", "chan", "sub"), None, None)),
        check_vma=False,
    )
```

```python
import functools
import math

import jax
import jax.numpy as jnp
from jax import lax
from jax.experimental import pallas as pl
from jax.experimental.pallas import tpu as pltpu
from jax.sharding import PartitionSpec as P

NCH = 128
TAPS = 12
SPEC = 8
BLOCKS = 4
BEAMS = 256


def filter_table(taps, chans):
    length = taps.shape[0]
    position = jnp.arange(length, dtype=jnp.int32) % chans
    channel = jnp.arange(chans, dtype=jnp.int32)
    phase = (position[:, None] * channel[None, :] % chans).astype(jnp.float32) * (
        2.0 * math.pi / chans
    )
    cosine = taps[:, None] * jnp.cos(phase)
    sine = taps[:, None] * jnp.sin(phase)
    upper = jnp.concatenate([cosine, -sine], axis=1)
    lower = jnp.concatenate([sine, cosine], axis=1)
    return jnp.concatenate([upper, lower], axis=0).astype(jnp.bfloat16)


def resynthesize(received, table, taps_count, chans):
    count = received.shape[0]
    spectra_n = received.shape[3]
    table3 = table.reshape(2 * taps_count * chans, 2, chans)
    grid = jnp.einsum("pcht,mch->ptm", received, table3, preferred_element_type=jnp.float32)
    grid = grid.reshape(count, spectra_n, 2, taps_count, chans)
    total = jnp.zeros((count, spectra_n + taps_count - 1, 2, chans), jnp.float32)
    for k in range(taps_count):
        total = total + jnp.pad(
            grid[:, :, :, k, :], ((0, 0), (k, taps_count - 1 - k), (0, 0), (0, 0))
        )
    return jnp.transpose(total, (0, 2, 1, 3)).reshape(
        count, 2, (spectra_n + taps_count - 1) * chans
    )


def local_plain(voltages, taps, input_id, counts, delays, beam_owner):
    n_chan = lax.axis_size("chan")
    n_sub = lax.axis_size("sub")
    inp_dev = voltages.shape[0]
    inputs = input_id.shape[0]
    chans = NCH
    taps_count = TAPS
    spectra_n = BLOCKS * SPEC
    ch_dev = chans // n_chan
    rows = inputs // n_sub
    section = BEAMS // n_sub
    most = min(section, max(2, 2 * section // n_chan))
    table = filter_table(taps, chans)
    position = jnp.arange(spectra_n, dtype=jnp.int32)
    valid = (position % SPEC < jnp.repeat(counts, SPEC)).astype(jnp.float32)
    total = jnp.sum(counts.astype(jnp.float32))
    frames = voltages.reshape(inp_dev, 2, spectra_n + taps_count - 1, chans)
    windows = jnp.concatenate(
        [frames[:, :, k : k + spectra_n, :] for k in range(taps_count)], axis=3
    )
    table3 = table.reshape(2, taps_count * chans, 2 * chans)
    filtered = jnp.einsum("icth,chm->mit", windows, table3, preferred_element_type=jnp.float32)
    filtered = filtered * valid[None, None, :]
    spectra = filtered.reshape(2, chans, inp_dev, spectra_n).astype(jnp.bfloat16)
    slot_of = jnp.zeros((inputs,), jnp.int32).at[input_id].set(jnp.arange(inputs, dtype=jnp.int32))
    turned = lax.all_to_all(spectra, "chan", split_axis=1, concat_axis=2, tiled=True)
    gathered = lax.all_gather(turned, "sub", axis=2, tiled=True)
    chan_part = slot_of // (n_sub * inp_dev)
    sub_part = slot_of // inp_dev % n_sub
    order = (sub_part * n_chan + chan_part) * inp_dev + slot_of % inp_dev
    by_id = jnp.take(gathered, order, axis=2)
    sub_index = lax.axis_index("sub")
    mine = lax.dynamic_slice_in_dim(by_id, sub_index * rows, rows, 2)
    real_part = jnp.einsum("cxit,cxjt->xij", mine, by_id, preferred_element_type=jnp.float32)
    imag_part = jnp.einsum("xit,xjt->xij", mine[1], by_id[0], preferred_element_type=jnp.float32)
    imag_part = imag_part - jnp.einsum(
        "xit,xjt->xij", mine[0], by_id[1], preferred_element_type=jnp.float32
    )
    visibility = (jnp.stack([real_part, imag_part], axis=1) / total).astype(jnp.bfloat16)
    channel = lax.axis_index("chan") * ch_dev + jnp.arange(ch_dev, dtype=jnp.int32)
    phase = (delays[None, :, :] * channel[:, None, None] % chans).astype(jnp.float32) * (
        2.0 * math.pi / chans
    )
    scale = 1.0 / math.sqrt(inputs)
    weight_cos = (jnp.cos(phase) * scale).astype(jnp.bfloat16)
    weight_sin = (jnp.sin(phase) * scale).astype(jnp.bfloat16)
    from_cos = jnp.einsum("xbi,cxit->cxbt", weight_cos, by_id, preferred_element_type=jnp.float32)
    from_sin = jnp.einsum("xbi,cxit->cxbt", weight_sin, by_id, preferred_element_type=jnp.float32)
    beams = jnp.stack([from_cos[0] - from_sin[1], from_cos[1] + from_sin[0]]).astype(jnp.bfloat16)
    owner = lax.dynamic_slice_in_dim(beam_owner[:, 0], sub_index * section, section)
    beam = jnp.arange(section, dtype=jnp.int32)
    earlier = (owner[None, :] == owner[:, None]) & (beam[None, :] < beam[:, None])
    rank = jnp.sum(earlier.astype(jnp.int32), axis=1)
    target = owner * most + rank
    select = (jnp.arange(n_chan * most, dtype=jnp.int32)[:, None] == target[None, :]).astype(
        jnp.bfloat16
    )
    placed = jnp.einsum("pb,cxbt->pcxt", select, beams, preferred_element_type=jnp.float32).astype(
        jnp.bfloat16
    )
    placed = placed.reshape(n_chan, most, 2, ch_dev, spectra_n)
    resynth = resynthesize(
        lax.all_to_all(placed, "chan", split_axis=0, concat_axis=3, tiled=True)[0],
        table,
        taps_count,
        chans,
    )
    return (visibility, resynth)


def filter_kernel(rows, pairs, steps, wide, n_chan, fr_ref, w_ref, mask_ref, out_ref):
    group = 4 if pairs % 4 == 0 else 1
    width = wide // n_chan
    for first in range(0, pairs, group):
        acc = jnp.zeros((group * rows, wide), jnp.float32)
        for k in range(steps):
            window = jnp.concatenate(
                [
                    jnp.concatenate([fr_ref[0, at], fr_ref[1, at]], axis=1)
                    for at in range(2 * first + k, 2 * (first + group) + k, 2)
                ],
                axis=0,
            )
            acc = acc + jnp.dot(window, w_ref[k], preferred_element_type=jnp.float32)
        for j in range(group):
            pair = first + j
            part = (acc[j * rows : (j + 1) * rows] * mask_ref[pair : pair + 1, :]).astype(
                jnp.bfloat16
            )
            for d in range(n_chan):
                out_ref[d, :, pair * width : (pair + 1) * width] = part[
                    :, d * width : (d + 1) * width
                ]


def channelize(voltages, taps, valid, n_chan):
    rows = voltages.shape[0]
    spectra_n = valid.shape[0]
    pairs = spectra_n // 2
    chans, ch_dev = NCH, NCH // n_chan
    steps = TAPS + 1
    frames_n = spectra_n + TAPS - 1
    frames = voltages.reshape(rows, 2, frames_n, chans)
    frames = jnp.transpose(frames, (1, 2, 0, 3))
    wide = 4 * chans
    column = jnp.arange(wide, dtype=jnp.int32)
    dest, rest = column // (4 * ch_dev), column % (4 * ch_dev)
    parity, part, inner = rest // (2 * ch_dev), rest // ch_dev % 2, rest % ch_dev
    channel = dest * ch_dev + inner
    row = jnp.arange(2 * chans, dtype=jnp.int32)
    phase = (row[:, None] % chans * channel[None, :] % chans).astype(jnp.float32) * (
        2.0 * math.pi / chans
    )
    cosine, sine = jnp.cos(phase), jnp.sin(phase)
    lower = row[:, None] >= chans
    trig = jnp.where(
        lower == (part[None, :] == 1), cosine, jnp.where(lower, sine, -sine)
    )
    trig = lax.optimization_barrier(trig)
    taps2 = taps.reshape(TAPS, chans)
    taps2 = jnp.concatenate([taps2, taps2], axis=1)
    even = jnp.pad(taps2, ((0, 1), (0, 0)))
    odd = jnp.pad(taps2, ((1, 0), (0, 0)))
    factor = jnp.where(parity[None, None, :] == 0, even[:, :, None], odd[:, :, None])
    weights = (trig[None] * factor).astype(jnp.bfloat16)
    mask = jnp.where(parity[None, :] == 0, valid[0::2, None], valid[1::2, None])
    return pl.pallas_call(
        functools.partial(filter_kernel, rows, pairs, steps, wide, n_chan),
        out_shape=jax.ShapeDtypeStruct((n_chan, rows, spectra_n * 2 * ch_dev), jnp.bfloat16),
        name="filterbank",
    )(frames, weights, mask)


def turn_of(steps):
    quarter = NCH // 4
    turn = steps & (NCH - 1)
    quadrant = (turn + quarter // 2) >> (quarter.bit_length() - 1)
    x = (turn - quadrant * quarter).astype(jnp.float32) * (2.0 * math.pi / NCH)
    y = x * x
    even = 1.0 + y * (-1 / 2 + y * (1 / 24 + y * (-1 / 720 + y * (1 / 40320))))
    odd = x * (1.0 + y * (-1 / 6 + y * (1 / 120 + y * (-1 / 5040 + y * (1 / 362880)))))
    swap = (quadrant & 1) == 1
    cosine, sine = jnp.where(swap, odd, even), jnp.where(swap, even, odd)
    cosine = jnp.where(((quadrant + 1) & 2) == 2, -cosine, cosine)
    return cosine, jnp.where((quadrant & 2) == 2, -sine, sine)


def weigh(first, scale, delay_ref, out_ref, at, left, high, wide):
    beams_n = delay_ref.shape[0]
    delay = delay_ref[at : at + high, left : left + wide]
    step_cos, step_sin = turn_of(delay)
    cosine, sine = turn_of(delay * first)

    def body(f, held):
        cosine, sine = held
        out_ref[f, at : at + high, left : left + wide] = cosine.astype(jnp.bfloat16)
        low = at + beams_n
        out_ref[f, low : low + high, left : left + wide] = sine.astype(jnp.bfloat16)
        return (
            cosine * step_cos - sine * step_sin,
            sine * step_cos + cosine * step_sin,
        )

    lax.fori_loop(0, out_ref.shape[0], body, (cosine * scale, sine * scale))


def turn_kernel(n_chan, n_sub, pieces, scale, x_ref, delay_ref, g_ref, weight_ref, own_sem, zs, zr, xs, xr, cs, cr):
    me_c, me_s = lax.axis_index("chan"), lax.axis_index("sub")
    core, across = me_s % 2, me_s // 2
    n_x = n_sub // 2
    twin = me_s + 1 - 2 * core
    rows = x_ref.shape[1] // pieces
    mesh_id = pl.DeviceIdType.MESH

    def chan_of(offset):
        return (me_c + offset) % n_chan

    def sub_of(offset):
        return (across + offset) % n_x * 2 + core

    barrier = pltpu.get_barrier_semaphore()
    for j in range(1, n_chan):
        pl.semaphore_signal(barrier, device_id={"chan": chan_of(j)}, device_id_type=mesh_id)
    for j in range(1, n_x):
        pl.semaphore_signal(barrier, device_id={"sub": sub_of(j)}, device_id_type=mesh_id)
    pl.semaphore_signal(barrier, device_id={"sub": twin}, device_id_type=mesh_id)
    pl.semaphore_wait(barrier, n_chan + n_x - 1)

    def place(ref, piece):
        return ref.at[piece * rows : (piece + 1) * rows]

    def z_copy(j, h):
        return pltpu.make_async_remote_copy(
            src_ref=place(x_ref.at[chan_of(j)], h),
            dst_ref=place(g_ref.at[me_s, me_c], h),
            send_sem=zs.at[j, h],
            recv_sem=zr.at[j, h],
            device_id={"chan": chan_of(j)},
            device_id_type=mesh_id,
        )

    def source(sub, j, h):
        if j == 0:
            return place(x_ref.at[me_c], h)
        return place(g_ref.at[sub, chan_of(n_chan - j)], h)

    def x_copy(dx, j, h):
        return pltpu.make_async_remote_copy(
            src_ref=source(me_s, j, h),
            dst_ref=place(g_ref.at[me_s, chan_of(n_chan - j)], h),
            send_sem=xs.at[dx, j, h],
            recv_sem=xr.at[dx, j, h],
            device_id={"sub": sub_of(dx)},
            device_id_type=mesh_id,
        )

    def core_copy(dx, j, h):
        home = sub_of(n_x - dx)
        block = place(g_ref.at[home, chan_of(n_chan - j)], h)
        return pltpu.make_async_remote_copy(
            src_ref=source(me_s, j, h) if dx == 0 else block,
            dst_ref=block,
            send_sem=cs.at[dx, j, h],
            recv_sem=cr.at[dx, j, h],
            device_id={"sub": twin},
            device_id_type=mesh_id,
        )

    own = pltpu.make_async_copy(x_ref.at[me_c], g_ref.at[me_s, me_c], own_sem)
    started = []
    for h in range(pieces):
        for j in range(1, n_chan):
            copy = z_copy(j, h)
            copy.start()
            started.append(copy)
    own.start()

    def spread(j, h):
        for dx in range(1, n_x):
            copy = x_copy(dx, j, h)
            copy.start()
            started.append(copy)
        copy = core_copy(0, j, h)
        copy.start()
        started.append(copy)

    for h in range(pieces):
        spread(0, h)
    ch_dev = weight_ref.shape[0]
    beams_n, inputs = delay_ref.shape
    high, wide = 16, 512
    units = [(at, left) for at in range(0, beams_n, high) for left in range(0, inputs, wide)]

    def work():
        if units:
            at, left = units.pop(0)
            weigh(me_c * ch_dev, scale, delay_ref, weight_ref, at, left, high, wide)

    def relay(h):
        for j in range(n_chan):
            work()
            for dx in range(1, n_x):
                x_copy(dx, j, h).wait_recv()
                copy = core_copy(dx, j, h)
                copy.start()
                started.append(copy)

    for h in range(pieces):
        for j in range(1, n_chan):
            work()
            z_copy(j, h).wait_recv()
            spread(j, h)
        if h > 0:
            relay(h - 1)
    relay(pieces - 1)
    while units:
        work()
    for h in range(pieces):
        for j in range(n_chan):
            for dx in range(n_x):
                core_copy(dx, j, h).wait_recv()
    for copy in started:
        copy.wait_send()
    own.wait()


def corner_turn(blocks, delays, n_chan, n_sub):
    pieces = 2
    dma = pltpu.SemaphoreType.DMA
    n_x = n_sub // 2
    beams_n, inputs = delays.shape
    return pl.pallas_call(
        functools.partial(turn_kernel, n_chan, n_sub, pieces, 1.0 / math.sqrt(inputs)),
        out_shape=[
            jax.ShapeDtypeStruct((n_sub,) + blocks.shape, jnp.bfloat16),
            jax.ShapeDtypeStruct((NCH // n_chan, 2 * beams_n, inputs), jnp.bfloat16),
        ],
        in_specs=[pl.BlockSpec(memory_space=pltpu.VMEM)] * 2,
        out_specs=[pl.BlockSpec(memory_space=pl.ANY), pl.BlockSpec(memory_space=pltpu.VMEM)],
        scratch_shapes=[
            dma,
            dma((n_chan, pieces)),
            dma((n_chan, pieces)),
            dma((n_x, n_chan, pieces)),
            dma((n_x, n_chan, pieces)),
            dma((n_x, n_chan, pieces)),
            dma((n_x, n_chan, pieces)),
        ],
        compiler_params=pltpu.CompilerParams(collective_id=0, has_side_effects=True),
        name="corner_turn",
    )(blocks, delays)


def beam_kernel(ch_dev, spectra_n, n_chan, batch, g_ref, perm_ref, weight_ref, sel_ref, id_ref, out_ref, held, ready, own_sem, send, recv):
    step = pl.program_id(0)
    pair = weight_ref.shape[0]
    steps = ch_dev // pair
    me_c = lax.axis_index("chan")
    mesh_id = pl.DeviceIdType.MESH

    @pl.when(step == 0)
    def _():
        barrier = pltpu.get_barrier_semaphore()
        for j in range(1, n_chan):
            pl.semaphore_signal(
                barrier, device_id={"chan": (me_c + j) % n_chan}, device_id_type=mesh_id
            )
        wide = min(256, g_ref.shape[1])

        @pl.loop(0, g_ref.shape[1] // wide)
        def _(m):
            at = pl.multiple_of(m * wide, wide)
            sorted_part = lax.dot_general(
                g_ref[:, pl.ds(at, wide)],
                perm_ref[...],
                (((0,), (0,)), ((), ())),
                preferred_element_type=jnp.float32,
            )
            per = 2 * ch_dev
            for q in range(wide // per):
                to = pl.multiple_of((m * (wide // per) + q) * (per + 8), 8)
                for tile in range(held.shape[0]):
                    held[tile, pl.ds(to, per), :] = sorted_part[
                        q * per : (q + 1) * per, tile * 128 : (tile + 1) * 128
                    ]

        pl.semaphore_wait(barrier, n_chan - 1)

    def rows_of(start):
        every = pl.ds(start, spectra_n, stride=2 * ch_dev + 8)
        return jnp.concatenate([held[tile, every, :] for tile in range(held.shape[0])], axis=1)

    def form(j):
        f = step * pair + j
        both = jnp.concatenate([rows_of(f), rows_of(f + ch_dev)], axis=0).astype(jnp.bfloat16)
        id_ref[j] = both
        mixed = lax.dot_general(
            weight_ref[j], both, (((1,), (1,)), ((), ())), preferred_element_type=jnp.float32
        )
        beams_n = mixed.shape[0] // 2
        upper, lower = mixed[:beams_n], mixed[beams_n:]
        beam_re = upper[:, :spectra_n] - lower[:, spectra_n:]
        beam_im = upper[:, spectra_n:] + lower[:, :spectra_n]
        return [beam_re, beam_im]

    beams = jnp.concatenate(form(0) + form(1), axis=1).astype(jnp.bfloat16)
    placed = jnp.dot(sel_ref[...], beams, preferred_element_type=jnp.float32).astype(jnp.bfloat16)
    most = placed.shape[0] // n_chan
    for d in range(n_chan):
        ready[d, step] = placed[d * most : (d + 1) * most]

    def copy_of(b, j):
        to = (me_c + j) % n_chan
        return pltpu.make_async_remote_copy(
            src_ref=ready.at[to, pl.ds(b * batch, batch)],
            dst_ref=out_ref.at[me_c, pl.ds(b * batch, batch)],
            send_sem=send.at[b, j],
            recv_sem=recv.at[b, j],
            device_id={"chan": to},
            device_id_type=mesh_id,
        )

    for b in range(steps // batch):

        @pl.when(step == (b + 1) * batch - 1)
        def _():
            for j in range(1, n_chan):
                copy_of(b, j).start()

    @pl.when(step == steps - 1)
    def _():
        own = pltpu.make_async_copy(ready.at[me_c], out_ref.at[me_c], own_sem)
        own.start()
        for b in range(steps // batch):
            for j in range(1, n_chan):
                copy_of(b, j).wait_recv()
        for b in range(steps // batch):
            for j in range(1, n_chan):
                copy_of(b, j).wait_send()
        own.wait()


def form_beams(gathered, perm, weights, select, spectra_n, n_chan):
    inputs = perm.shape[0]
    ch_dev, double_n, _ = weights.shape
    slots, beams_n = select.shape
    cols = gathered.shape[1]
    pair = 2
    steps = ch_dev // pair
    batch = steps // 4
    dma = pltpu.SemaphoreType.DMA
    whole = lambda shape: pl.BlockSpec(
        shape, lambda f: (0,) * len(shape), pipeline_mode=pl.Buffered(1)
    )
    travel = (n_chan, steps, slots // n_chan, 2 * pair * spectra_n)
    return pl.pallas_call(
        functools.partial(beam_kernel, ch_dev, spectra_n, n_chan, batch),
        grid=(steps,),
        in_specs=[
            whole((inputs, cols)),
            whole((inputs, inputs)),
            pl.BlockSpec((pair, double_n, inputs), lambda f: (f, 0, 0)),
            whole((slots, beams_n)),
        ],
        out_specs=[
            pl.BlockSpec((pair, 2 * spectra_n, inputs), lambda f: (f, 0, 0)),
            pl.BlockSpec(memory_space=pl.ANY),
        ],
        scratch_shapes=[
            pltpu.VMEM((inputs // 128, cols + 8 * spectra_n, 128), jnp.float32),
            pltpu.VMEM(travel, jnp.bfloat16),
            dma,
            dma((4, n_chan)),
            dma((4, n_chan)),
        ],
        out_shape=[
            jax.ShapeDtypeStruct((ch_dev, 2 * spectra_n, inputs), jnp.bfloat16),
            jax.ShapeDtypeStruct(travel, jnp.bfloat16),
        ],
        compiler_params=pltpu.CompilerParams(
            dimension_semantics=("arbitrary",), collective_id=1, has_side_effects=True
        ),
        name="beams",
    )(gathered, perm, weights, select)


def visibility_kernel(sub_ref, scale_ref, left_ref, right_ref, out_ref):
    for j in range(left_ref.shape[0]):
        left = left_ref[j]
        half, rows = left.shape[0] // 2, left.shape[1]
        turned = jnp.concatenate([left[half:], -left[:half]], axis=0)
        both = jnp.concatenate([left, turned], axis=1)
        product = lax.dot_general(
            both, right_ref[j], (((0,), (0,)), ((), ())), preferred_element_type=jnp.float32
        )
        product = (product * scale_ref[0]).astype(jnp.bfloat16)
        out_ref[j, 0] = product[:rows]
        out_ref[j, 1] = product[rows:]


def correlate(by_id, scale, sub_index, rows):
    ch_dev, depth, inputs = by_id.shape
    group = 2 if ch_dev % 2 == 0 else 1
    return pl.pallas_call(
        visibility_kernel,
        grid_spec=pltpu.PrefetchScalarGridSpec(
            num_scalar_prefetch=1,
            grid=(ch_dev // group,),
            in_specs=[
                pl.BlockSpec(memory_space=pltpu.SMEM),
                pl.BlockSpec((group, depth, rows), lambda f, s: (f, 0, s[0])),
                pl.BlockSpec((group, depth, inputs), lambda f, s: (f, 0, 0)),
            ],
            out_specs=pl.BlockSpec((group, 2, rows, inputs), lambda f, s: (f, 0, 0, 0)),
        ),
        out_shape=jax.ShapeDtypeStruct((ch_dev, 2, rows, inputs), jnp.bfloat16),
        cost_estimate=pl.CostEstimate(
            flops=4 * ch_dev * rows * inputs * depth,
            bytes_accessed=4 * ch_dev * rows * inputs,
            transcendentals=0,
        ),
        name="visibility",
    )(sub_index, scale, by_id, by_id)


def voice_kernel(spectra_n, count, frames_n, b_ref, w_ref, out_ref):
    chans = w_ref.shape[2] // 2
    group = 4
    for first in range(0, frames_n, group):
        size = min(group, frames_n - first)
        acc = jnp.zeros((size * count, w_ref.shape[2]), jnp.float32)
        for k in range(TAPS):
            low = first - k
            if low + size <= 0 or low >= spectra_n:
                continue
            start = (low + TAPS - 1) * count
            acc = acc + jnp.dot(
                b_ref[start : start + size * count, :], w_ref[k], preferred_element_type=jnp.float32
            )
        for j in range(size):
            at = (first + j) * chans
            for c in range(2):
                out_ref[:, c, at : at + chans] = acc[
                    j * count : (j + 1) * count, c * chans : (c + 1) * chans
                ]


def synthesize(received, taps):
    n_chan, steps, count, width = received.shape
    spectra_n = BLOCKS * SPEC
    pair = width // (2 * spectra_n)
    chans = n_chan * steps * pair
    frames_n = spectra_n + TAPS - 1
    bank = received.reshape(n_chan * steps, count, pair, 2, spectra_n)
    bank = jnp.transpose(bank, (4, 1, 3, 0, 2)).reshape(spectra_n, count, 2 * chans)
    bank = jnp.pad(bank, ((TAPS - 1, TAPS - 1), (0, 0), (0, 0))).reshape(-1, 2 * chans)
    index = jnp.arange(2 * chans, dtype=jnp.int32)
    inner = index % chans
    phase = (inner[:, None] * inner[None, :] % chans).astype(jnp.float32) * (2.0 * math.pi / chans)
    cosine, sine = jnp.cos(phase), jnp.sin(phase)
    from_im, to_im = index[:, None] >= chans, index[None, :] >= chans
    trig = jnp.where(from_im == to_im, cosine, jnp.where(to_im, sine, -sine))
    trig = lax.optimization_barrier(trig)
    taps2 = taps.reshape(TAPS, 1, chans)
    weights = (trig[None] * jnp.concatenate([taps2, taps2], axis=2)).astype(jnp.bfloat16)
    return pl.pallas_call(
        functools.partial(voice_kernel, spectra_n, count, frames_n),
        out_shape=jax.ShapeDtypeStruct((count, 2, frames_n * chans), jnp.float32),
        name="voices",
    )(bank, weights)


def local(voltages, taps, input_id, counts, delays, beam_owner):
    n_chan = lax.axis_size("chan")
    n_sub = lax.axis_size("sub")
    inp_dev = voltages.shape[0]
    inputs = input_id.shape[0]
    chans = NCH
    spectra_n = BLOCKS * SPEC
    ch_dev = chans // n_chan
    rows = inputs // n_sub
    section = BEAMS // n_sub
    most = min(section, max(2, 2 * section // n_chan))
    if inp_dev % 32 or 4 * ch_dev % 128 or rows % 128 or n_sub % 2 or most % 16:
        return local_plain(voltages, taps, input_id, counts, delays, beam_owner)
    position = jnp.arange(spectra_n, dtype=jnp.int32)
    valid = (position % SPEC < jnp.repeat(counts, SPEC)).astype(jnp.float32)
    total = jnp.sum(counts.astype(jnp.float32))
    sub_index = lax.axis_index("sub")
    blocks = channelize(voltages, taps, valid, n_chan)
    gathered, weights = corner_turn(blocks, delays, n_chan, n_sub)
    gathered = gathered.reshape(inputs, -1)
    names = jnp.transpose(input_id.reshape(n_chan, n_sub, inp_dev), (1, 0, 2)).reshape(inputs)
    perm = (names[:, None] == jnp.arange(inputs, dtype=jnp.int32)[None, :]).astype(jnp.bfloat16)
    owner = lax.dynamic_slice_in_dim(beam_owner[:, 0], sub_index * section, section)
    beam = jnp.arange(section, dtype=jnp.int32)
    earlier = (owner[None, :] == owner[:, None]) & (beam[None, :] < beam[:, None])
    rank = jnp.sum(earlier.astype(jnp.int32), axis=1)
    target = owner * most + rank
    select = (jnp.arange(n_chan * most, dtype=jnp.int32)[:, None] == target[None, :]).astype(
        jnp.bfloat16
    )
    by_id, received = form_beams(gathered, perm, weights, select, spectra_n, n_chan)
    visibility = correlate(by_id, (1.0 / total)[None], sub_index.astype(jnp.int32)[None], rows)
    resynth = synthesize(received, taps)
    return (visibility, resynth)


def solution(mesh):
    placed = (
        P(("grp", "chan", "sub"), None, None),
        P(),
        P(),
        P("grp"),
        P(("grp", "sub"), None),
        P("grp", None),
    )
    return jax.shard_map(
        local,
        mesh=mesh,
        in_specs=placed,
        out_specs=(P(("grp", "chan"), None, "sub", None), P(("grp", "chan", "sub"), None, None)),
        check_vma=False,
    )
```
